32 devices in a mesh: expert: 16 (over z, y, core), dp: 2 (over x).
Axes of the slice: x: 2, y: 2, z: 4, core: 2. Of those that a mesh axis runs over, the one named last changes fastest.
Arguments:
- tokens: bfloat16 [2, 2048, 1024], P(None, ('expert', 'dp')), may hold values from -6 to 6
- routes: int32 [2, 2048, 6], P(None, ('expert', 'dp')), may hold values from 0 to 15, all different within a row; in each aligned block of 64 rows (0 to 63, 64 to 127, ..., all dimensions but the last counted through in order) at most 32 rows name the same one
- gate_weights: float32 [2, 2048, 6], P(None, ('expert', 'dp')), may hold values from 0.05 to 0.35
- cotangent: bfloat16 [2, 2048, 1024], P(None, ('expert', 'dp')), may hold values from -6 to 6
- expert_plan: int32 [16], replicated, may hold values from 0 to 15, each once
- weight_in: bfloat16 [16, 1024, 1536], P('expert', 'dp'), may hold values from -0.1875 to 0.1875
- weight_out: bfloat16 [16, 768, 1024], P('expert', 'dp'), may hold values from -0.21875 to 0.21875
- first_in: float32 [16, 1024, 1536], P('expert', 'dp'), may hold values from -6 to 6
- second_in: float32 [16, 1024, 1536], P('expert', 'dp'), may hold values from 0.5 to 20
- first_out: float32 [16, 768, 1024], P('expert', 'dp'), may hold values from -6 to 6
- second_out: float32 [16, 768, 1024], P('expert', 'dp'), may hold values from 0.5 to 20
Outputs:
- layer_output: bfloat16 [2, 2048, 1024], P(None, ('expert', 'dp'))
- token_gradient: bfloat16 [2, 2048, 1024], P(None, ('expert', 'dp'))
- weight_in_next: bfloat16 [16, 1024, 1536], P('expert', 'dp')
- weight_out_next: bfloat16 [16, 768, 1024], P('expert', 'dp')
- first_in_next: float32 [16, 1024, 1536], P('expert', 'dp')
- second_in_next: float32 [16, 1024, 1536], P('expert', 'dp')
- first_out_next: float32 [16, 768, 1024], P('expert', 'dp')
- second_out_next: float32 [16, 768, 1024], P('expert', 'dp')
The draws below stay inside these ranges and needn't reach their ends.
Inputs may be any that keep to these rules, and one draw needn't show every extreme that they name: `routes`: each row names 6 different experts. In the 64 rows of one device in one micro-batch (an aligned block), no expert is named by more than 32 rows; in some blocks one expert is named by exactly 32 rows. A permutation. Before the migration, index d of the expert axis holds expert d; after it, expert expert_plan[d].
All inputs are finite; a program needn't handle non-finite values.
Results may differ from the reference program's by a relative error of at most 0.014.
Values may be sent and summed in bfloat16 or wider, within the bound.
A program may use at most 128 MiB of HBM per device.

```python
import math
import jax
import jax.numpy as jnp
import numpy as np
from jax import lax

D = 1024
FF = 768
TOP = 6
MICRO = 2
TOK_MB = 64
EXPERTS = 16
CAP = 32
TOKENS = 2048
N_EXPERT = 16
N_DP = 2


def level_of(own_key, shape, split, smallest, top_value):
    def one(axis_at, blocks):
        steps = jax.random.uniform(jax.random.fold_in(jax.random.fold_in(own_key, 6), axis_at), (blocks,), jnp.float32, smallest / len(split), top_value / len(split))
        return jnp.repeat(jnp.exp(steps), shape[axis_at] // blocks).reshape((-1,) + (1,) * (len(shape) - axis_at - 1))

    gain = one(*split[0])
    for cut in split[1:]:
        gain = gain * one(*cut)
    return gain


def shared_out(rng, own, number, rows, amount, top, reach, slope):
    ranking = jax.random.permutation(rng, amount)
    crowded, ordinary = portions_of(amount, rows * top, reach, slope, True), portions_of(amount, rows * top, reach, slope, False)
    places = jnp.arange(amount)

    def named(lengths, turn):
        used = int((lengths > 0).sum())
        fixed = max(1, used // 4)
        passed = fixed + (places - fixed + turn * (used - fixed)) % max(1, amount - fixed)
        return jnp.zeros((amount,), jnp.int32).at[ranking[jnp.where(places < fixed, places, passed)]].set(jnp.asarray(lengths, jnp.int32))

    lengths = jnp.where(number % 4 == 0, named(crowded, number // 4), named(ordinary, number - number // 4 - 1))
    mixed = jax.random.permutation(jax.random.fold_in(own, 3), amount)
    source_of, sink = mixed[0:amount // 2 * 2:2], mixed[1:amount // 2 * 2:2]
    room = jnp.minimum(lengths[source_of] - 1, reach - lengths[sink]) // 2
    room = jnp.where((source_of == ranking[0]) | (sink == ranking[0]) | (lengths[sink] == 0), 0, jnp.maximum(room, 0))
    passed = jax.random.randint(jax.random.fold_in(own, 4), (amount // 2,), 0, 1 << 20) % (room + 1)
    lengths = lengths.at[source_of].add(-passed).at[sink].add(passed)
    members = jnp.searchsorted(jnp.cumsum(lengths), jnp.arange(rows * top), side="right").astype(jnp.int32)
    listing = members.reshape(top, rows).T
    listing = listing[jax.random.permutation(jax.random.fold_in(own, 1), rows)]
    turn = jax.random.randint(jax.random.fold_in(own, 2), (rows, 1), 0, top)
    return jnp.take_along_axis(listing, (jnp.arange(top)[None, :] + turn) % top, axis=1)


def portions_of(amount, total, most, skew, full):
    loads = [(1 << 20) // math.isqrt(standing ** skew) + 1 for standing in range(1, amount + 1)]
    largest = most if full else min(most, max(-(-total // amount), total * loads[0] // sum(loads)))
    least = 1 if total - largest >= amount - 1 else 0
    given, surplus = [largest] + [least] * (amount - 1), total - largest - least * (amount - 1)
    while surplus > 0:
        free = [i for i in range(1, amount) if given[i] < largest] or [i for i in range(1, amount) if given[i] < most]
        pool, budget = sum([loads[i] for i in free]), surplus
        for i in free:
            addition = min(most - given[i], max(1, budget * loads[i] // pool), surplus)
            given[i] = given[i] + addition
            surplus = surplus - addition
    return np.array(given)


def centred(rng, dims, scale, most, cuts=(), kind=jnp.bfloat16):
    array = jax.random.normal(rng, dims, jnp.float32) * scale
    if len(cuts) > 0:
        array = level_of(rng, dims, cuts, -0.22, 0.18) * array
    return jnp.clip(array, min=-most, max=most).astype(kind)


def setup_inputs(seed: int = 0) -> dict:
    key_of = jax.random.split(jax.random.key(seed), 12)
    tokens = centred(key_of[0], (MICRO, TOKENS, D), 1.0, 6.0, ((1, 32),))
    routes_keys = jax.random.split(jax.random.fold_in(key_of[1], 1), MICRO * TOKENS // TOK_MB)
    routes_turns = jax.random.permutation(jax.random.fold_in(key_of[1], 3), MICRO * TOKENS // TOK_MB)
    routes = jax.vmap(lambda own, number: shared_out(jax.random.fold_in(key_of[1], 2), own, number, TOK_MB, EXPERTS, TOP, CAP, 2))(routes_keys, routes_turns).reshape((MICRO, TOKENS, TOP))
    gate_weights = jnp.clip(0.05 + 0.29999999 * jax.random.uniform(key_of[2], (MICRO, TOKENS, TOP), jnp.float32) ** level_of(key_of[2], (MICRO, TOKENS, TOP), ((1, 32),), -0.2, 0.2), 0.05, 0.35)
    cotangent = centred(key_of[3], (MICRO, TOKENS, D), 1.0, 6.0, ((1, 32),))
    expert_plan = jax.random.permutation(key_of[4], EXPERTS).astype(jnp.int32)
    weight_in = centred(key_of[5], (EXPERTS, D, 2 * FF), D ** -0.5, 0.1875, ((0, 16), (1, 2)))
    weight_out = centred(key_of[6], (EXPERTS, FF, D), FF ** -0.5, 0.21875, ((0, 16), (1, 2)))
    first_in = centred(key_of[7], (EXPERTS, D, 2 * FF), 1.0, 6.0, ((0, 16), (1, 2)), jnp.float32)
    second_in = jnp.clip(jnp.exp(math.log(20.0) - 3.6888795 * jax.random.uniform(key_of[8], (EXPERTS, D, 2 * FF), jnp.float32) ** level_of(key_of[8], (EXPERTS, D, 2 * FF), ((0, 16), (1, 2)), -0.2, 0.2)), 0.5, 20.0)
    first_out = centred(key_of[9], (EXPERTS, FF, D), 1.0, 6.0, ((0, 16), (1, 2)), jnp.float32)
    second_out = jnp.clip(jnp.exp(math.log(20.0) - 3.6888795 * jax.random.uniform(key_of[10], (EXPERTS, FF, D), jnp.float32) ** level_of(key_of[10], (EXPERTS, FF, D), ((0, 16), (1, 2)), -0.2, 0.2)), 0.5, 20.0)
    return {"tokens": tokens, "routes": routes, "gate_weights": gate_weights, "cotangent": cotangent, "expert_plan": expert_plan, "weight_in": weight_in, "weight_out": weight_out, "first_in": first_in, "second_in": second_in, "first_out": first_out, "second_out": second_out}


beta_one = 0.9
beta_two = 0.95
learn_rate = 0.00042
decay_rate = 0.1
epsilon = 1e-08
steps_done = 10

def slot_ranks(chosen):
    hits = (chosen[..., None] == jnp.arange(EXPERTS, dtype=jnp.int32)).astype(jnp.int32)
    per_token = lax.optimization_barrier(jnp.sum(hits, axis=3))
    before = jnp.cumsum(per_token, axis=2) - per_token
    return lax.optimization_barrier(jnp.sum(hits * before[:, :, :, None, :], axis=4)).astype(jnp.int32)

def expert_pass(rows, grads, weight_first, weight_second):
    pre = jnp.dot(rows, weight_first, preferred_element_type=jnp.float32)
    gate_part = pre[:, :FF]
    up_part = pre[:, FF:]
    sigma = jax.nn.sigmoid(gate_part)
    hidden = (gate_part * sigma * up_part).astype(jnp.bfloat16)
    output = jnp.dot(hidden, weight_second, preferred_element_type=jnp.float32).astype(jnp.bfloat16)
    hidden_grad = lax.dot_general(grads, weight_second, (((1,), (1,)), ((), ())), preferred_element_type=jnp.float32)
    pre_grad = jnp.concatenate([hidden_grad * up_part * sigma * (1.0 + gate_part * (1.0 - sigma)), hidden_grad * gate_part * sigma], axis=1).astype(jnp.bfloat16)
    grad_first = lax.dot_general(rows, pre_grad, (((0,), (0,)), ((), ())), preferred_element_type=jnp.float32)
    grad_second = lax.dot_general(hidden, grads, (((0,), (0,)), ((), ())), preferred_element_type=jnp.float32)
    token_part = lax.dot_general(pre_grad, weight_first, (((1,), (1,)), ((), ())), preferred_element_type=jnp.float32).astype(jnp.bfloat16)
    return (output, token_part, grad_first, grad_second)

def adam_update(weight, gradient, first, second):
    first_new = beta_one * first + (1.0 - beta_one) * gradient
    second_new = beta_two * second + (1.0 - beta_two) * gradient * gradient
    ratio = first_new / (1.0 - beta_one ** steps_done) / (jnp.sqrt(second_new / (1.0 - beta_two ** steps_done)) + epsilon)
    master = weight.astype(jnp.float32)
    return ((master - learn_rate * (ratio + decay_rate * master)).astype(jnp.bfloat16), first_new, second_new)

def reference(tokens, routes, gate_weights, cotangent, expert_plan, weight_in, weight_out, first_in, second_in, first_out, second_out):
    blocks = N_EXPERT * N_DP
    inputs = tokens.reshape(MICRO, blocks, TOK_MB, D)
    chosen = routes.reshape(MICRO, blocks, TOK_MB, TOP)
    gates = gate_weights.reshape(MICRO, blocks, TOK_MB, TOP)
    upstream = cotangent.reshape(MICRO, blocks, TOK_MB, D)
    ranks = slot_ranks(chosen)
    micro_index = jnp.broadcast_to(jnp.arange(MICRO, dtype=jnp.int32)[:, None, None, None], chosen.shape)
    block_index = jnp.broadcast_to(jnp.arange(blocks, dtype=jnp.int32)[None, :, None, None], chosen.shape)
    spread = jnp.broadcast_to(inputs[:, :, :, None, :], chosen.shape + (D,))
    sent = jnp.zeros((EXPERTS, MICRO, blocks, CAP, D), jnp.bfloat16).at[chosen, micro_index, block_index, ranks].set(spread)
    scaled = (gates[..., None] * upstream[:, :, :, None, :].astype(jnp.float32)).astype(jnp.bfloat16)
    sent_grad = jnp.zeros((EXPERTS, MICRO, blocks, CAP, D), jnp.bfloat16).at[chosen, micro_index, block_index, ranks].set(scaled)

    def per_expert(expert):
        rows = sent[expert].reshape(MICRO, N_EXPERT, N_DP, CAP, D)
        grads = sent_grad[expert].reshape(MICRO, N_EXPERT, N_DP, CAP, D)
        weight_first = weight_in[expert]
        weight_second = weight_out[expert]
        outputs = []
        backs = []
        total_first = jnp.zeros((D, 2 * FF), jnp.float32)
        total_second = jnp.zeros((FF, D), jnp.float32)
        for replica in range(N_DP):
            mine = rows[:, :, replica].reshape(-1, D)
            mine_grad = grads[:, :, replica].reshape(-1, D)
            output, token_part, grad_first, grad_second = expert_pass(mine, mine_grad, weight_first, weight_second)
            outputs.append(output.reshape(MICRO, N_EXPERT, CAP, D))
            backs.append(token_part.reshape(MICRO, N_EXPERT, CAP, D))
            total_first = total_first + lax.optimization_barrier(grad_first.astype(jnp.bfloat16)).astype(jnp.float32)
            total_second = total_second + lax.optimization_barrier(grad_second.astype(jnp.bfloat16)).astype(jnp.float32)
        outputs = jnp.stack(outputs, axis=2).reshape(MICRO, blocks, CAP, D)
        backs = jnp.stack(backs, axis=2).reshape(MICRO, blocks, CAP, D)
        return (outputs, backs, total_first, total_second)
    outputs, backs, grad_in, grad_out = lax.map(per_expert, jnp.arange(EXPERTS, dtype=jnp.int32))
    picked = outputs[chosen, micro_index, block_index, ranks]
    layer_output = lax.optimization_barrier(jnp.sum(gates[..., None] * picked.astype(jnp.float32), axis=3)).astype(jnp.bfloat16).reshape(MICRO, TOKENS, D)
    picked_grad = backs[chosen, micro_index, block_index, ranks]
    token_gradient = lax.optimization_barrier(jnp.sum(picked_grad.astype(jnp.float32), axis=3)).astype(jnp.bfloat16).reshape(MICRO, TOKENS, D)
    new_in, first_in_new, second_in_new = adam_update(weight_in, grad_in, first_in, second_in)
    new_out, first_out_new, second_out_new = adam_update(weight_out, grad_out, first_out, second_out)
    return (layer_output, token_gradient, jnp.take(new_in, expert_plan, axis=0), jnp.take(new_out, expert_plan, axis=0), jnp.take(first_in_new, expert_plan, axis=0), jnp.take(second_in_new, expert_plan, axis=0), jnp.take(first_out_new, expert_plan, axis=0), jnp.take(second_out_new, expert_plan, axis=0))
```

```python
import jax
import jax.numpy as jnp
from jax import lax
from jax.sharding import PartitionSpec as P

beta_one = 0.9
beta_two = 0.95
learn_rate = 0.00042
decay_rate = 0.1
epsilon = 1e-08
steps_done = 10


def adam_update(weight, gradient, first, second):
    first_new = beta_one * first + (1.0 - beta_one) * gradient
    second_new = beta_two * second + (1.0 - beta_two) * gradient * gradient
    ratio = (
        first_new
        / (1.0 - beta_one**steps_done)
        / (jnp.sqrt(second_new / (1.0 - beta_two**steps_done)) + epsilon)
    )
    master = weight.astype(jnp.float32)
    return (
        (master - learn_rate * (ratio + decay_rate * master)).astype(jnp.bfloat16),
        first_new,
        second_new,
    )


def spread_pieces(block, count):
    rows = block.shape[1] // count
    pieces = block.astype(jnp.bfloat16).reshape(count, rows, block.shape[2])
    return lax.all_to_all(pieces, "expert", split_axis=0, concat_axis=0, tiled=True)


def land_pieces(spread, expert_plan, shape):
    picked = jnp.take(spread, expert_plan, axis=0, mode="clip")
    return lax.all_to_all(picked, "expert", split_axis=0, concat_axis=0, tiled=True).reshape(shape)


def on_device(
    tokens,
    routes,
    gate_weights,
    cotangent,
    expert_plan,
    weight_in,
    weight_out,
    first_in,
    second_in,
    first_out,
    second_out,
):
    count = lax.axis_size("expert")
    micro_count, token_count, width = tokens.shape
    top_count = routes.shape[2]
    row_count = micro_count * token_count

    own_routes = routes.reshape(row_count, top_count)
    own_gates = gate_weights.reshape(row_count, top_count)
    hits = own_routes[None, :, :] == expert_plan[:, None, None]
    sent_gates = jnp.sum(jnp.where(hits, own_gates[None, :, :], 0.0), axis=2)
    gate_column = lax.all_to_all(
        sent_gates, "expert", split_axis=0, concat_axis=0, tiled=True
    ).reshape(count * row_count, 1)
    rows = lax.all_gather(tokens.reshape(row_count, width), "expert", axis=0, tiled=True)
    upstream = lax.all_gather(cotangent.reshape(row_count, width), "expert", axis=0, tiled=True)

    spread_in = spread_pieces(weight_in, count)
    spread_out = spread_pieces(weight_out, count)
    own_in = land_pieces(spread_in, expert_plan, weight_in.shape)
    own_out = land_pieces(spread_out, expert_plan, weight_out.shape)
    whole_in = lax.all_gather(own_in[0], "dp", axis=0, tiled=True)
    whole_out = lax.all_gather(own_out[0], "dp", axis=0, tiled=True)
    hidden_width = whole_out.shape[0]

    moments = (first_in, second_in, first_out, second_out)
    spread_moments = [spread_pieces(member, count) for member in moments]
    landed = [
        land_pieces(spread, expert_plan, member.shape)
        for spread, member in zip(spread_moments, moments)
    ]

    pre = jnp.dot(rows, whole_in, preferred_element_type=jnp.float32)
    gate_part = pre[:, :hidden_width]
    up_part = pre[:, hidden_width:]
    sigma = jax.nn.sigmoid(gate_part)
    hidden = (gate_part * sigma * up_part).astype(jnp.bfloat16)
    output = jnp.dot(hidden, whole_out, preferred_element_type=jnp.float32)
    weighted = (gate_column * output).astype(jnp.bfloat16)
    layer_rows = lax.psum_scatter(weighted, "expert", scatter_dimension=0, tiled=True)

    scaled = (gate_column * upstream.astype(jnp.float32)).astype(jnp.bfloat16)
    hidden_grad = lax.dot_general(
        scaled, whole_out, (((1,), (1,)), ((), ())), preferred_element_type=jnp.float32
    )
    pre_grad = jnp.concatenate(
        [
            hidden_grad * up_part * sigma * (1.0 + gate_part * (1.0 - sigma)),
            hidden_grad * gate_part * sigma,
        ],
        axis=1,
    ).astype(jnp.bfloat16)
    grad_in = lax.dot_general(
        rows, pre_grad, (((0,), (0,)), ((), ())), preferred_element_type=jnp.float32
    ).astype(jnp.bfloat16)
    grad_out = lax.dot_general(
        hidden, scaled, (((0,), (0,)), ((), ())), preferred_element_type=jnp.float32
    ).astype(jnp.bfloat16)
    token_part = lax.dot_general(
        pre_grad, whole_in, (((1,), (1,)), ((), ())), preferred_element_type=jnp.float32
    ).astype(jnp.bfloat16)
    token_rows = lax.psum_scatter(token_part, "expert", scatter_dimension=0, tiled=True)
    share_in = lax.psum_scatter(grad_in, "dp", scatter_dimension=0, tiled=True)
    share_out = lax.psum_scatter(grad_out, "dp", scatter_dimension=0, tiled=True)

    first_in, second_in, first_out, second_out = [m.astype(jnp.float32) for m in landed]
    new_in, first_in_new, second_in_new = adam_update(
        own_in, share_in.astype(jnp.float32)[None], first_in, second_in
    )
    new_out, first_out_new, second_out_new = adam_update(
        own_out, share_out.astype(jnp.float32)[None], first_out, second_out
    )
    return (
        layer_rows.reshape(tokens.shape),
        token_rows.reshape(tokens.shape),
        new_in,
        new_out,
        first_in_new,
        second_in_new,
        first_out_new,
        second_out_new,
    )


def solution(mesh):
    placed = (
        P(None, ("expert", "dp"), None),
        P(None, ("expert", "dp"), None),
        P(None, ("expert", "dp"), None),
        P(None, ("expert", "dp"), None),
        P(),
        P("expert", "dp", None),
        P("expert", "dp", None),
        P("expert", "dp", None),
        P("expert", "dp", None),
        P("expert", "dp", None),
        P("expert", "dp", None),
    )
    return jax.shard_map(
        on_device,
        mesh=mesh,
        in_specs=placed,
        out_specs=(
            P(None, ("expert", "dp"), None),
            P(None, ("expert", "dp"), None),
            P("expert", "dp", None),
            P("expert", "dp", None),
            P("expert", "dp", None),
            P("expert", "dp", None),
            P("expert", "dp", None),
            P("expert", "dp", None),
        ),
        check_vma=False,
    )
```

```python
import jax
import jax.numpy as jnp
from jax import lax
from jax.experimental.layout import Layout, with_layout_constraint
from jax.sharding import PartitionSpec as P

beta_one = 0.9
beta_two = 0.95
learn_rate = 0.00042
decay_rate = 0.1
epsilon = 1e-08
steps_done = 10


def adam_update(weight, gradient, first, second):
    first_new = beta_one * first + (1.0 - beta_one) * gradient
    second_new = beta_two * second + (1.0 - beta_two) * gradient * gradient
    ratio = (
        first_new
        / (1.0 - beta_one**steps_done)
        / (jnp.sqrt(second_new / (1.0 - beta_two**steps_done)) + epsilon)
    )
    master = weight.astype(jnp.float32)
    return (
        (master - learn_rate * (ratio + decay_rate * master)).astype(jnp.bfloat16),
        first_new,
        second_new,
    )


def exchange(pieces):
    return lax.all_to_all(pieces, "expert", split_axis=0, concat_axis=0, tiled=True)


def cut(block, count):
    return block.astype(jnp.bfloat16).reshape(count, block.shape[1] // count, block.shape[2])


def pick(spread, expert_plan):
    return jnp.take(spread, expert_plan, axis=0, mode="clip")


def tie(*values):
    return lax.optimization_barrier(values)


def row_major(value):
    return with_layout_constraint(value, Layout(major_to_minor=tuple(range(value.ndim))))


def on_device(
    tokens,
    routes,
    gate_weights,
    cotangent,
    expert_plan,
    weight_in,
    weight_out,
    first_in,
    second_in,
    first_out,
    second_out,
):
    count = lax.axis_size("expert")
    micro_count, token_count, width = tokens.shape
    top_count = routes.shape[2]
    row_count = micro_count * token_count

    own_routes = routes.reshape(row_count, top_count)
    own_gates = gate_weights.reshape(row_count, top_count)
    hits = own_routes[None, :, :] == expert_plan[:, None, None]
    sent_gates = jnp.sum(jnp.where(hits, own_gates[None, :, :], 0.0), axis=2)
    gate_column = lax.all_to_all(
        sent_gates, "expert", split_axis=0, concat_axis=0, tiled=True
    ).reshape(count * row_count, 1)
    rows = lax.all_gather(tokens.reshape(row_count, width), "expert", axis=0, tiled=True)
    upstream = lax.all_gather(cotangent.reshape(row_count, width), "expert", axis=0, tiled=True)

    pieces, gate_column = tie(cut(weight_in, count), gate_column)
    spread_in = exchange(pieces)
    pieces, spread_in = tie(cut(weight_out, count), spread_in)
    spread_out = exchange(pieces)
    pieces, spread_out = tie(pick(spread_in, expert_plan), spread_out)
    own_in = exchange(pieces).reshape(weight_in.shape)
    pieces, own_in = tie(pick(spread_out, expert_plan), own_in)
    own_out = exchange(pieces).reshape(weight_out.shape)
    own_in, rows, upstream = tie(own_in, rows, upstream)
    whole_in = lax.all_gather(own_in[0], "dp", axis=0, tiled=True)
    pieces, own_out = tie(cut(first_in, count), own_out)
    whole_out = lax.all_gather(own_out[0], "dp", axis=0, tiled=True)
    hidden_width = whole_out.shape[0]

    spread_one = exchange(pieces)
    pre = jnp.dot(rows, whole_in, preferred_element_type=jnp.float32)
    pieces, spread_one, pre = tie(cut(second_in, count), spread_one, pre)
    spread_two = exchange(pieces)

    gate_part = pre[:, :hidden_width]
    up_part = pre[:, hidden_width:]
    sigma = jax.nn.sigmoid(gate_part)
    hidden = (gate_part * sigma * up_part).astype(jnp.bfloat16)
    scaled = (gate_column * upstream.astype(jnp.float32)).astype(jnp.bfloat16)
    hidden_grad = lax.dot_general(
        scaled, whole_out, (((1,), (1,)), ((), ())), preferred_element_type=jnp.float32
    )
    pre_grad = jnp.concatenate(
        [
            hidden_grad * up_part * sigma * (1.0 + gate_part * (1.0 - sigma)),
            hidden_grad * gate_part * sigma,
        ],
        axis=1,
    ).astype(jnp.bfloat16)
    output = jnp.dot(hidden, whole_out, preferred_element_type=jnp.float32)
    weighted = (gate_column * output).astype(jnp.bfloat16)
    pieces, spread_two, weighted, late_in = tie(
        cut(first_out, count), spread_two, weighted, whole_in
    )
    spread_three = exchange(pieces)
    layer_rows = lax.psum_scatter(weighted, "expert", scatter_dimension=0, tiled=True)

    token_part = lax.dot_general(
        pre_grad, late_in, (((1,), (1,)), ((), ())), preferred_element_type=jnp.float32
    ).astype(jnp.bfloat16)
    pieces, spread_three, token_part, late_rows = tie(
        cut(second_out, count), spread_three, token_part, rows
    )
    spread_four = exchange(pieces)
    token_rows = lax.psum_scatter(token_part, "expert", scatter_dimension=0, tiled=True)
    grad_in = row_major(
        lax.dot_general(
            late_rows, pre_grad, (((0,), (0,)), ((), ())), preferred_element_type=jnp.float32
        ).astype(jnp.bfloat16)
    )
    pieces, spread_four, grad_in, late_upstream = tie(
        pick(spread_one, expert_plan), spread_four, grad_in, upstream
    )
    landed_one = exchange(pieces)
    share_in = lax.psum_scatter(grad_in, "dp", scatter_dimension=0, tiled=True)
    scaled = (gate_column * late_upstream.astype(jnp.float32)).astype(jnp.bfloat16)
    grad_out = row_major(
        lax.dot_general(
            hidden, scaled, (((0,), (0,)), ((), ())), preferred_element_type=jnp.float32
        ).astype(jnp.bfloat16)
    )
    pieces, landed_one, grad_out = tie(pick(spread_two, expert_plan), landed_one, grad_out)
    landed_two = exchange(pieces)
    share_out = lax.psum_scatter(grad_out, "dp", scatter_dimension=0, tiled=True)
    pieces, landed_two = tie(pick(spread_three, expert_plan), landed_two)
    landed_three = exchange(pieces)
    pieces, landed_three = tie(pick(spread_four, expert_plan), landed_three)
    landed_four = exchange(pieces)

    new_in, first_in_new, second_in_new = adam_update(
        own_in,
        share_in.astype(jnp.float32)[None],
        landed_one.reshape(first_in.shape).astype(jnp.float32),
        landed_two.reshape(second_in.shape).astype(jnp.float32),
    )
    new_out, first_out_new, second_out_new = adam_update(
        own_out,
        share_out.astype(jnp.float32)[None],
        landed_three.reshape(first_out.shape).astype(jnp.float32),
        landed_four.reshape(second_out.shape).astype(jnp.float32),
    )
    return (
        layer_rows.reshape(tokens.shape),
        token_rows.reshape(tokens.shape),
        new_in,
        new_out,
        first_in_new,
        second_in_new,
        first_out_new,
        second_out_new,
    )


def solution(mesh):
    placed = (
        P(None, ("expert", "dp"), None),
        P(None, ("expert", "dp"), None),
        P(None, ("expert", "dp"), None),
        P(None, ("expert", "dp"), None),
        P(),
        P("expert", "dp", None),
        P("expert", "dp", None),
        P("expert", "dp", None),
        P("expert", "dp", None),
        P("expert", "dp", None),
        P("expert", "dp", None),
    )
    return jax.shard_map(
        on_device,
        mesh=mesh,
        in_specs=placed,
        out_specs=(
            P(None, ("expert", "dp"), None),
            P(None, ("expert", "dp"), None),
            P("expert", "dp", None),
            P("expert", "dp", None),
            P("expert", "dp", None),
            P("expert", "dp", None),
            P("expert", "dp", None),
            P("expert", "dp", None),
        ),
        check_vma=False,
    )
```

```python
import jax
import jax.numpy as jnp
from jax import lax
from jax.experimental.layout import Layout, with_layout_constraint
from jax.sharding import PartitionSpec as P

beta_one = 0.9
beta_two = 0.95
learn_rate = 0.00042
decay_rate = 0.1
epsilon = 1e-08
steps_done = 10


def adam_update(weight, gradient, first, second):
    first_new = beta_one * first + (1.0 - beta_one) * gradient
    second_new = beta_two * second + (1.0 - beta_two) * gradient * gradient
    ratio = (
        first_new
        / (1.0 - beta_one**steps_done)
        / (jnp.sqrt(second_new / (1.0 - beta_two**steps_done)) + epsilon)
    )
    master = weight.astype(jnp.float32)
    return (
        (master - learn_rate * (ratio + decay_rate * master)).astype(jnp.bfloat16),
        first_new,
        second_new,
    )


def exchange(pieces):
    return lax.all_to_all(pieces, "expert", split_axis=0, concat_axis=0, tiled=True)


def cut(block, count):
    return block.astype(jnp.bfloat16).reshape(count, block.shape[1] // count, block.shape[2])


def pick(spread, expert_plan):
    return jnp.take(spread, expert_plan, axis=0, mode="clip")


def tie(*values):
    return lax.optimization_barrier(values)


def row_major(value):
    return with_layout_constraint(value, Layout(major_to_minor=tuple(range(value.ndim))))


def on_device(
    tokens,
    routes,
    gate_weights,
    cotangent,
    expert_plan,
    weight_in,
    weight_out,
    first_in,
    second_in,
    first_out,
    second_out,
):
    count = lax.axis_size("expert")
    micro_count, token_count, width = tokens.shape
    top_count = routes.shape[2]
    row_count = micro_count * token_count

    own_routes = routes.reshape(row_count, top_count)
    own_gates = gate_weights.reshape(row_count, top_count)
    hits = own_routes[None, :, :] == expert_plan[:, None, None]
    sent_gates = jnp.sum(jnp.where(hits, own_gates[None, :, :], 0.0), axis=2)
    all_gates = lax.all_gather(sent_gates, "expert", axis=0, tiled=False)
    gate_column = lax.dynamic_index_in_dim(
        all_gates, lax.axis_index("expert"), axis=1, keepdims=False
    ).reshape(count * row_count, 1)
    rows = lax.all_gather(tokens.reshape(row_count, width), "expert", axis=0, tiled=True)
    upstream = lax.all_gather(cotangent.reshape(row_count, width), "expert", axis=0, tiled=True)

    spread_in = exchange(cut(weight_in, count))
    pieces, spread_in = tie(cut(weight_out, count), spread_in)
    spread_out = exchange(pieces)
    pieces, spread_out = tie(pick(spread_in, expert_plan), spread_out)
    own_in = exchange(pieces).reshape(weight_in.shape)
    pieces, own_in = tie(pick(spread_out, expert_plan), own_in)
    own_out = exchange(pieces).reshape(weight_out.shape)
    own_in, rows, upstream = tie(own_in, rows, upstream)
    whole_in = lax.all_gather(own_in[0], "dp", axis=0, tiled=True)
    pieces, own_out = tie(cut(first_in, count), own_out)
    whole_out = lax.all_gather(own_out[0], "dp", axis=0, tiled=True)
    hidden_width = whole_out.shape[0]

    spread_one = exchange(pieces)
    pre = jnp.dot(rows, whole_in, preferred_element_type=jnp.float32)
    pieces, spread_one, pre = tie(cut(second_in, count), spread_one, pre)
    spread_two = exchange(pieces)

    gate_part = pre[:, :hidden_width]
    up_part = pre[:, hidden_width:]
    sigma = jax.nn.sigmoid(gate_part)
    hidden = (gate_part * sigma * up_part).astype(jnp.bfloat16)
    scaled = (gate_column * upstream.astype(jnp.float32)).astype(jnp.bfloat16)
    hidden_grad = lax.dot_general(
        scaled, whole_out, (((1,), (1,)), ((), ())), preferred_element_type=jnp.float32
    )
    pre_grad = jnp.concatenate(
        [
            hidden_grad * up_part * sigma * (1.0 + gate_part * (1.0 - sigma)),
            hidden_grad * gate_part * sigma,
        ],
        axis=1,
    ).astype(jnp.bfloat16)
    output = jnp.dot(hidden, whole_out, preferred_element_type=jnp.float32)
    weighted = (gate_column * output).astype(jnp.bfloat16)
    pieces, spread_two, weighted, late_in = tie(
        cut(first_out, count), spread_two, weighted, whole_in
    )
    spread_three = exchange(pieces)
    layer_rows = lax.psum_scatter(weighted, "expert", scatter_dimension=0, tiled=True)

    token_part = lax.dot_general(
        pre_grad, late_in, (((1,), (1,)), ((), ())), preferred_element_type=jnp.float32
    ).astype(jnp.bfloat16)
    pieces, spread_three, token_part, late_rows = tie(
        cut(second_out, count), spread_three, token_part, rows
    )
    spread_four = exchange(pieces)
    token_rows = lax.psum_scatter(token_part, "expert", scatter_dimension=0, tiled=True)
    grad_in = row_major(
        lax.dot_general(
            late_rows, pre_grad, (((0,), (0,)), ((), ())), preferred_element_type=jnp.float32
        ).astype(jnp.bfloat16)
    )
    pieces, spread_four, grad_in, late_upstream = tie(
        pick(spread_one, expert_plan), spread_four, grad_in, upstream
    )
    landed_one = exchange(pieces)
    grad_in, layer_rows = tie(grad_in, layer_rows)
    share_in = lax.psum_scatter(grad_in, "dp", scatter_dimension=0, tiled=True)
    scaled = (gate_column * late_upstream.astype(jnp.float32)).astype(jnp.bfloat16)
    grad_out = row_major(
        lax.dot_general(
            hidden, scaled, (((0,), (0,)), ((), ())), preferred_element_type=jnp.float32
        ).astype(jnp.bfloat16)
    )
    pieces, landed_one, grad_out, layer_rows = tie(
        pick(spread_two, expert_plan), landed_one, grad_out, layer_rows
    )
    landed_two = exchange(pieces)
    share_out = lax.psum_scatter(grad_out, "dp", scatter_dimension=0, tiled=True)
    pieces, landed_two = tie(pick(spread_three, expert_plan), landed_two)
    landed_three = exchange(pieces)
    pieces, landed_three, token_rows = tie(
        pick(spread_four, expert_plan), landed_three, token_rows
    )
    landed_four = exchange(pieces)

    new_in, first_in_new, second_in_new = adam_update(
        own_in,
        share_in.astype(jnp.float32)[None],
        landed_one.reshape(first_in.shape).astype(jnp.float32),
        landed_two.reshape(second_in.shape).astype(jnp.float32),
    )
    new_out, first_out_new, second_out_new = adam_update(
        own_out,
        share_out.astype(jnp.float32)[None],
        landed_three.reshape(first_out.shape).astype(jnp.float32),
        landed_four.reshape(second_out.shape).astype(jnp.float32),
    )
    return (
        layer_rows.reshape(tokens.shape),
        token_rows.reshape(tokens.shape),
        new_in,
        new_out,
        first_in_new,
        second_in_new,
        first_out_new,
        second_out_new,
    )


def solution(mesh):
    placed = (
        P(None, ("expert", "dp"), None),
        P(None, ("expert", "dp"), None),
        P(None, ("expert", "dp"), None),
        P(None, ("expert", "dp"), None),
        P(),
        P("expert", "dp", None),
        P("expert", "dp", None),
        P("expert", "dp", None),
        P("expert", "dp", None),
        P("expert", "dp", None),
        P("expert", "dp", None),
    )
    return jax.shard_map(
        on_device,
        mesh=mesh,
        in_specs=placed,
        out_specs=(
            P(None, ("expert", "dp"), None),
            P(None, ("expert", "dp"), None),
            P("expert", "dp", None),
            P("expert", "dp", None),
            P("expert", "dp", None),
            P("expert", "dp", None),
            P("expert", "dp", None),
            P("expert", "dp", None),
        ),
        check_vma=False,
    )
```
